32 devices in a mesh: rep: 4 (over z), shard: 8 (over y, x, core).
Axes of the slice: x: 2, y: 2, z: 4, core: 2. Of those that a mesh axis runs over, the one named last changes fastest.
Arguments:
- inputs: bfloat16 [65536, 768], P(('rep', 'shard')), may hold values from -6 to 6
- cotangent: bfloat16 [65536, 768], P(('rep', 'shard')), may hold values from -6 to 6
- picture_ids: int32 [65536], P(('rep', 'shard')), may hold values from 0 to 19, as said below
- picture_lengths: int32 [32, 20], P(('rep', 'shard')), may hold values from 0 to 1024, as said below
- picture_offsets: int32 [32, 20], P(('rep', 'shard')), may hold values from 0 to 2048, as said below
- padding: int32 [65536], P(('rep', 'shard')), may hold values from 0 to 1, as said below
- ln1_gain: bfloat16 [768], P('shard'), may hold values from 0.099609375 to 1.8984375
- ln1_bias: bfloat16 [768], P('shard'), may hold values from -4 to 4
- qkv_weight: bfloat16 [768, 2304], P('shard'), may hold values from -0.21875 to 0.21875
- qkv_bias: bfloat16 [2304], P('shard'), may hold values from -4 to 4
- query_gain: bfloat16 [64], P('shard'), may hold values from 0.099609375 to 1.8984375
- key_gain: bfloat16 [64], P('shard'), may hold values from 0.099609375 to 1.8984375
- out_weight: bfloat16 [768, 768], P('shard'), may hold values from -0.875 to 0.875
- out_bias: bfloat16 [768], P('shard'), may hold values from -4 to 4
- ln2_gain: bfloat16 [768], P('shard'), may hold values from 0.099609375 to 1.8984375
- ln2_bias: bfloat16 [768], P('shard'), may hold values from -4 to 4
- up_weight: bfloat16 [768, 3072], P('shard'), may hold values from -0.21875 to 0.21875
- up_bias: bfloat16 [3072], P('shard'), may hold values from -4 to 4
- down_weight: bfloat16 [3072, 768], P('shard'), may hold values from -0.109375 to 0.109375
- down_bias: bfloat16 [768], P('shard'), may hold values from -4 to 4
Outputs:
- output: bfloat16 [65536, 768], P(('rep', 'shard'))
- input_grad: float32 [65536, 768], P(('rep', 'shard'))
- ln1_gain_grad: float32 [768], P('shard')
- ln1_bias_grad: float32 [768], P('shard')
- qkv_weight_grad: float32 [768, 2304], P('shard')
- qkv_bias_grad: float32 [2304], P('shard')
- query_gain_grad: float32 [64], P('shard')
- key_gain_grad: float32 [64], P('shard')
- out_weight_grad: float32 [768, 768], P('shard')
- out_bias_grad: float32 [768], P('shard')
- ln2_gain_grad: float32 [768], P('shard')
- ln2_bias_grad: float32 [768], P('shard')
- up_weight_grad: float32 [768, 3072], P('shard')
- up_bias_grad: float32 [3072], P('shard')
- down_weight_grad: float32 [3072, 768], P('shard')
- down_bias_grad: float32 [768], P('shard')
The draws below stay inside these ranges and needn't reach their ends.
Inputs may be any that keep to these rules, and one draw needn't show every extreme that they name: `picture_lengths`: each row's pictures lie end to end from position 0; slots after a row's last picture have length 0 and offset 2048; every picture has 100 to 1024 patches; one row holds a picture of 1024, another 20 pictures of 100. `picture_offsets`: the first position of each picture in its row; 2048 for empty slots. `picture_ids`: each patch names the slot of the picture that holds it; a padding slot names the slot after the row's last picture, at most 19. `padding`: 1 exactly on the positions covered by the row's pictures.
All inputs are finite; a program needn't handle non-finite values.
Results may differ from the reference program's by a relative error of at most 0.019.
Values may be sent and summed in bfloat16 or wider, within the bound.
No kernel may reach another device: no remote copies, remote signals or barrier semaphores. Data moves between devices by JAX's collectives and lax.ppermute only.
A program may use at most 320 MiB of HBM per device.

```python
import jax
import jax.numpy as jnp
from jax import lax

D = 768
HEADS = 12
HD = 64
FF = 3072
PACK = 2048
MINPIC = 100
MAXPIC = 1024
PICS = 20
ROWS = 32
TOKENS = 65536


def packed_layout(key):
    base_key = jax.random.fold_in(key, 7)
    drawn = jax.random.randint(base_key, (ROWS, PICS), MINPIC, MAXPIC + 1, dtype=jnp.int32)
    drawn = drawn.at[0, 0].set(MAXPIC)
    drawn = drawn.at[ROWS - 1].set(MINPIC)
    ends = jnp.cumsum(drawn, axis=1).astype(jnp.int32)
    kept = ends <= PACK
    lengths = jnp.where(kept, drawn, 0).astype(jnp.int32)
    used_rows = jnp.sum(lengths, axis=1, keepdims=True).astype(jnp.int32)
    offsets = jnp.where(kept, ends - drawn, PACK).astype(jnp.int32)
    positions = jnp.arange(PACK, dtype=jnp.int32)
    kept_ends = jnp.where(kept, ends, PACK + 1)
    slot_of = jnp.sum((kept_ends[:, None, :] <= positions[None, :, None]).astype(jnp.int32), axis=2)
    slot_of = jnp.minimum(slot_of, PICS - 1).astype(jnp.int32)
    living = (positions[None, :] < used_rows).astype(jnp.int32)
    return (slot_of.reshape(-1), lengths, offsets, living.reshape(-1))


def draw_picture_ids(key, part):
    return packed_layout(key)[0]


def draw_picture_lengths(key, part):
    return packed_layout(key)[1]


def draw_picture_offsets(key, part):
    return packed_layout(key)[2]


def draw_padding(key, part):
    return packed_layout(key)[3]


def strengthened(entries, own_key, source, target, blocks, factor):
    owner, partner = [(jnp.arange(entries.shape[dim]) // (entries.shape[dim] // blocks)).reshape([-1 if axis == dim else 1 for axis in range(entries.ndim)]) for dim in (source, target)]
    chosen = jax.random.permutation(own_key, blocks)[partner]
    strong = (owner == chosen) | (owner == (partner + blocks // 2) % blocks)
    return jnp.where(strong, factor * entries, entries)


def level_of(rng, dims, cuts, least, largest):
    def one(dim, blocks):
        steps = jax.random.uniform(jax.random.fold_in(jax.random.fold_in(rng, 6), dim), (blocks,), jnp.float32, least / len(cuts), largest / len(cuts))
        return jnp.repeat(jnp.exp(steps), dims[dim] // blocks).reshape((-1,) + (1,) * (len(dims) - dim - 1))

    gain = one(*cuts[0])
    for cut in cuts[1:]:
        gain = gain * one(*cut)
    return gain


def normal_values(own_key, dims, scale, reach, split=(), kind=jnp.bfloat16):
    entries = scale * jax.random.normal(own_key, dims, jnp.float32)
    if split:
        entries = entries * level_of(own_key, dims, split, -0.22, 0.18)
    return jnp.clip(entries, -reach, reach).astype(kind)


def gaussian_with(own_key, extent, deviation, reach, shards, heavy, kind=jnp.bfloat16):
    values = deviation * jax.random.normal(own_key, extent, jnp.float32)
    if shards:
        values = values * level_of(own_key, extent, shards, -0.22, 0.18)
    return jnp.clip(strengthened(values, jax.random.fold_in(own_key, 3), *heavy), -reach, reach).astype(kind)


def setup_inputs(seed: int = 0) -> dict:
    key_of = jax.random.split(jax.random.key(seed), 21)
    return {
        "inputs": normal_values(key_of[0], (TOKENS, D), 1.0, 6.0, ((0, 32),)),
        "cotangent": gaussian_with(key_of[1], (TOKENS, D), 1.0, 6.0, ((0, 32),), (0, 1, 32, 2.75)),
        "picture_ids": draw_picture_ids(jax.random.fold_in(key_of[20], 71), 0),
        "picture_lengths": draw_picture_lengths(jax.random.fold_in(key_of[20], 71), 0),
        "picture_offsets": draw_picture_offsets(jax.random.fold_in(key_of[20], 71), 0),
        "padding": draw_padding(jax.random.fold_in(key_of[20], 71), 0),
        "ln1_gain": jnp.clip(1.0 + 0.18 * jax.random.normal(key_of[6], (D,), jnp.float32), 0.099609375, 1.8984375).astype(jnp.bfloat16),
        "ln1_bias": normal_values(key_of[7], (D,), 0.3, 4.0, ((0, 8),)),
        "qkv_weight": normal_values(key_of[8], (D, 3 * D), D ** -0.5, 0.21875, ((0, 8),)),
        "qkv_bias": normal_values(key_of[9], (3 * D,), 0.5, 4.0, ((0, 8),)),
        "query_gain": jnp.clip(1.0 + 0.18 * jax.random.normal(key_of[10], (HD,), jnp.float32), 0.099609375, 1.8984375).astype(jnp.bfloat16),
        "key_gain": jnp.clip(1.0 + 0.18 * jax.random.normal(key_of[11], (HD,), jnp.float32), 0.099609375, 1.8984375).astype(jnp.bfloat16),
        "out_weight": normal_values(key_of[12], (D, D), (D // 16) ** -0.5, 0.875, ((0, 8),)),
        "out_bias": normal_values(key_of[13], (D,), 0.5, 4.0, ((0, 8),)),
        "ln2_gain": jnp.clip(1.0 + 0.18 * jax.random.normal(key_of[14], (D,), jnp.float32), 0.099609375, 1.8984375).astype(jnp.bfloat16),
        "ln2_bias": normal_values(key_of[15], (D,), 0.3, 4.0, ((0, 8),)),
        "up_weight": normal_values(key_of[16], (D, FF), D ** -0.5, 0.21875, ((0, 8),)),
        "up_bias": normal_values(key_of[17], (FF,), 0.5, 4.0, ((0, 8),)),
        "down_weight": normal_values(key_of[18], (FF, D), FF ** -0.5, 0.109375, ((0, 8),)),
        "down_bias": normal_values(key_of[19], (D,), 0.5, 4.0, ((0, 8),)),
    }


@jax.custom_vjp
def low(v):
    return lax.optimization_barrier(v.astype(jnp.bfloat16)).astype(jnp.float32)

@jax.custom_vjp
def low_back(v):
    return v

def low_keep(v):
    return (low(v), None)

def low_pass(kept, grad):
    return (grad,)

def back_keep(v):
    return (v, None)

def back_low(kept, grad):
    return (low(grad),)
low.defvjp(low_keep, low_pass)
low_back.defvjp(back_keep, back_low)
NEG_FILL = -1e+30
NORM_EPS = 1e-06
HIGH = lax.Precision.HIGHEST

def layer_norm(values, gain_vec, shift_vec):
    center = values - lax.optimization_barrier(jnp.mean(values, axis=-1, keepdims=True))
    spread = lax.optimization_barrier(jnp.mean(center * center, axis=-1, keepdims=True))
    return center * lax.rsqrt(spread + NORM_EPS) * gain_vec + shift_vec

def head_norm(values, gain_vec):
    center = values - lax.optimization_barrier(jnp.mean(values, axis=-1, keepdims=True))
    spread = lax.optimization_barrier(jnp.mean(center * center, axis=-1, keepdims=True))
    return center * lax.rsqrt(spread + NORM_EPS) * gain_vec

def windows(row_ids, row_lengths, row_offsets):
    slot_ids = jnp.arange(row_lengths.shape[-1], dtype=jnp.int32)
    matches = row_ids[..., :, None] == slot_ids
    window_start = lax.optimization_barrier(jnp.sum(jnp.where(matches, row_offsets[..., None, :], 0), axis=-1)).astype(jnp.int32)
    window_stop = window_start + lax.optimization_barrier(jnp.sum(jnp.where(matches, row_lengths[..., None, :], 0), axis=-1)).astype(jnp.int32)
    return (window_start, window_stop)

def allowed_block(first_row, start_blk, stop_blk, live_blk, live_row):
    key_pos = jnp.arange(live_row.shape[0], dtype=jnp.int32)
    query_pos = first_row + jnp.arange(start_blk.shape[0], dtype=jnp.int32)
    inside = (key_pos[None, :] >= start_blk[:, None]) & (key_pos[None, :] < stop_blk[:, None])
    living = (live_blk[:, None] > 0) & (live_row[None, :] > 0)
    return inside & living | (key_pos[None, :] == query_pos[:, None])

def row_forward(params, row_input, row_ids, row_lengths, row_offsets, row_padding):
    gain_one, shift_one, weight_qkv, bias_qkv, gain_query, gain_key, weight_out, bias_out, gain_two, shift_two, weight_up, bias_up, weight_down, bias_down = params
    tok_count = row_input.shape[0]
    normed = low(layer_norm(row_input, gain_one, shift_one))
    qkv_all = low_back(jnp.dot(normed, weight_qkv, precision=HIGH) + bias_qkv)
    head_view = qkv_all.reshape(tok_count, 3, HEADS, HD)
    queries = low(head_norm(head_view[:, 0], gain_query) * HD ** (-0.5))
    key_heads = low(head_norm(head_view[:, 1], gain_key))
    values = low(head_view[:, 2])
    window_start, window_stop = windows(row_ids, row_lengths, row_offsets)
    block_rows = min(512, tok_count)

    def one_block(first_row):
        query_blk = lax.dynamic_slice_in_dim(queries, first_row, block_rows, 0)
        allowed = allowed_block(first_row, lax.dynamic_slice_in_dim(window_start, first_row, block_rows, 0), lax.dynamic_slice_in_dim(window_stop, first_row, block_rows, 0), lax.dynamic_slice_in_dim(row_padding, first_row, block_rows, 0), row_padding)
        scores = low_back(jnp.einsum('qhd,khd->hqk', query_blk, key_heads, precision=HIGH))
        scores = jnp.where(allowed[None], scores, NEG_FILL)
        row_max = lax.optimization_barrier(jnp.max(scores, axis=-1, keepdims=True))
        exponent = jnp.exp(scores - row_max)
        shares = low(exponent / lax.optimization_barrier(jnp.sum(exponent, axis=-1, keepdims=True)))
        return jnp.einsum('hqk,khd->qhd', shares, values, precision=HIGH)
    block_starts = jnp.arange(tok_count // block_rows, dtype=jnp.int32) * block_rows
    attended = lax.map(jax.checkpoint(one_block), block_starts).reshape(tok_count, D)
    mixed = low(low_back(attended))
    attn_branch = low_back(jnp.dot(mixed, weight_out, precision=HIGH) + bias_out)
    hidden = row_input + attn_branch
    normed_two = low(layer_norm(hidden, gain_two, shift_two))
    up_proj = low_back(jnp.dot(normed_two, weight_up, precision=HIGH) + bias_up)
    activated = low(jax.nn.gelu(up_proj, approximate=False))
    mlp_branch = low_back(jnp.dot(activated, weight_down, precision=HIGH) + bias_down)
    return hidden + mlp_branch

def reference(inputs, cotangent, picture_ids, picture_lengths, picture_offsets, padding, ln1_gain, ln1_bias, qkv_weight, qkv_bias, query_gain, key_gain, out_weight, out_bias, ln2_gain, ln2_bias, up_weight, up_bias, down_weight, down_bias):
    params = tuple((element.astype(jnp.float32) for element in (ln1_gain, ln1_bias, qkv_weight, qkv_bias, query_gain, key_gain, out_weight, out_bias, ln2_gain, ln2_bias, up_weight, up_bias, down_weight, down_bias)))
    row_count = picture_lengths.shape[0]
    tok_count = inputs.shape[0] // row_count
    row_inputs = inputs.astype(jnp.float32).reshape(row_count, tok_count, D)
    row_ids = picture_ids.reshape(row_count, tok_count)
    row_padding = padding.reshape(row_count, tok_count)
    checked_row = jax.checkpoint(row_forward)

    def forward(param_set, layer_input):

        def row_step(carried, pieces):
            result = checked_row(param_set, pieces[0], pieces[1], pieces[2], pieces[3], pieces[4])
            return (carried, result)
        _, outputs = lax.scan(row_step, jnp.zeros((), jnp.float32), (layer_input, row_ids, picture_lengths, picture_offsets, row_padding))
        return outputs
    outputs, pullback = jax.vjp(forward, params, row_inputs)
    weighted = cotangent.astype(jnp.float32) * padding.astype(jnp.float32)[:, None]
    param_grads, input_grads = pullback(weighted.reshape(row_count, tok_count, D))
    return (outputs.reshape(-1, D).astype(jnp.bfloat16), input_grads.reshape(-1, D), param_grads[0], param_grads[1], param_grads[2], param_grads[3], param_grads[4], param_grads[5], param_grads[6], param_grads[7], param_grads[8], param_grads[9], param_grads[10], param_grads[11], param_grads[12], param_grads[13])
```

```python
import jax
import jax.numpy as jnp
from jax import lax
from jax.experimental import pallas as pl
from jax.experimental.pallas import tpu as pltpu
from jax.sharding import PartitionSpec as P

HEADS = 12
HD = 64
NORM_EPS = 1e-06
LOG2E = 1.4426950408889634
LN2 = 0.6931471805599453
FAR = 512.0
CONST_LANE = 127
BLK = 256
MAX_BLOCKS = 5
VMEM_LIMIT = 60 * 1024 * 1024

F32 = jnp.float32
BF16 = jnp.bfloat16

NT = (((1,), (1,)), ((), ()))
NN = (((1,), (0,)), ((), ()))
TN = (((0,), (0,)), ((), ()))


def dot(lhs, rhs, dims=NN):
    return lax.dot_general(lhs, rhs, dims, preferred_element_type=F32)


def params(**kw):
    return pltpu.CompilerParams(vmem_limit_bytes=VMEM_LIMIT, **kw)


def row_stats(values):
    mean = jnp.mean(values, axis=-1, keepdims=True)
    center = values - mean
    rstd = lax.rsqrt(jnp.mean(center * center, axis=-1, keepdims=True) + NORM_EPS)
    return center * rstd, rstd


def const_spec(shape):
    return pl.BlockSpec(shape, lambda *_: (0,) * len(shape), pipeline_mode=pl.Buffered(1))


def qkv_kernel(x_ref, g_ref, b_ref, w_ref, wb_ref, gq_ref, gk_ref, avg_ref,
               n_ref, q_ref, k_ref, v_ref, rq_ref, rk_ref):
    z, _ = row_stats(x_ref[...].astype(F32))
    normed = (z * g_ref[...] + b_ref[...]).astype(BF16)
    n_ref[...] = normed
    width = q_ref.shape[1]
    avg = avg_ref[...]
    for part in range(3):
        for col in range(0, width, 256):
            at = part * width + col
            pre = dot(normed, w_ref[:, at:at + 256]) + wb_ref[:, at:at + 256]
            if part == 2:
                v_ref[:, col:col + 256] = pre.astype(BF16)
                continue
            high = pre.astype(BF16)
            low = (pre - high.astype(F32)).astype(BF16)
            center = pre - (dot(high, avg) + dot(low, avg))
            rstd = lax.rsqrt(dot((center * center).astype(BF16), avg) + NORM_EPS)
            gain = gk_ref if part else gq_ref
            out = k_ref if part else q_ref
            rout = rk_ref if part else rq_ref
            out[:, col:col + 256] = (center * rstd * gain[:, col:col + 256]).astype(BF16)
            rout[:, col:col + 256] = rstd.astype(BF16)


def qkv_project(x, gain, bias, weight, wbias, gain_q, gain_k, avg):
    total, width = x.shape
    rows = 512
    tile = pl.BlockSpec((rows, width), lambda i: (i, 0))
    outs = [jax.ShapeDtypeStruct((total, width), BF16)] * 6
    return pl.pallas_call(
        qkv_kernel,
        grid=(total // rows,),
        in_specs=[tile, const_spec((1, width)), const_spec((1, width)), const_spec(weight.shape),
                  const_spec((1, 3 * width)), const_spec((1, width)), const_spec((1, width)),
                  const_spec((256, 256))],
        out_specs=[tile] * 6,
        out_shape=outs,
        compiler_params=params(),
        name="qkv_project",
    )(x, gain, bias, weight, wbias, gain_q, gain_k, avg)


def half_masks(rows):
    lane = lax.broadcasted_iota(jnp.int32, (rows, 2 * HD), 1)
    return lane < HD


def for_each_picture(len_ref, off_ref, total, body):
    slots = len_ref.shape[0]

    def one(slot, carry):
        length = len_ref[slot]
        start = off_ref[slot]

        @pl.when(length > 0)
        def _():
            aligned = start // 16 * 16
            count = (start + length - aligned + BLK - 1) // BLK
            for blocks in range(1, MAX_BLOCKS + 1):
                @pl.when(count == blocks)
                def _():
                    first = pl.multiple_of(jnp.minimum(aligned, total - blocks * BLK), 16)
                    body(slot, start, start + length, first, blocks)
        return carry

    lax.fori_loop(0, slots, one, 0)


def inside_rows(first, start, stop, rows, width):
    at = first + lax.broadcasted_iota(jnp.int32, (rows, width), 0)
    return (at >= start) & (at < stop)


def stacked_heads(block, left):
    zero = jnp.zeros_like(block)
    return jnp.concatenate([jnp.where(left, block, zero), jnp.where(left, zero, block)], axis=0)


def slot_lanes(slot, rows):
    lane = lax.broadcasted_iota(jnp.int32, (rows, 128), 1)
    return (lane == slot) | (lane == CONST_LANE)


def fwd_kernel(len_ref, off_ref, q_ref, k_ref, v_ref, aq_ref, ak_ref, o_ref, l_ref):
    total = q_ref.shape[0]
    o_ref[...] = v_ref[...]
    l_ref[...] = jnp.zeros_like(l_ref)
    left = half_masks(BLK)
    one = jnp.ones((BLK, 128), BF16)

    def picture(slot, start, stop, first, blocks):
        span = blocks * BLK
        keys = jnp.concatenate([k_ref[pl.ds(first, span), :], ak_ref[pl.ds(first, span), :]], axis=1)
        vals = v_ref[pl.ds(first, span), :]
        left_all = half_masks(span)
        ones_all = jnp.ones((span, 128), BF16)
        vals = jnp.concatenate([stacked_heads(vals, left_all), stacked_heads(ones_all, left_all)], axis=1)

        def step(j, carry):
            at = pl.multiple_of(first + j * BLK, 16)
            code = jnp.where(slot_lanes(slot, BLK), aq_ref[pl.ds(at, BLK), :], jnp.zeros((), BF16))
            query = stacked_heads(q_ref[pl.ds(at, BLK), :], left)
            query = jnp.concatenate([query, jnp.concatenate([code, code], axis=0)], axis=1)
            shares = jnp.exp2(dot(query, keys, NT)).astype(BF16)
            shares = jnp.concatenate([shares[:BLK], shares[BLK:]], axis=1)
            mixed = dot(shares, vals)
            keep = inside_rows(at, start, stop, BLK, 128)
            inv = 1.0 / mixed[:, 128:]
            o_ref[pl.ds(at, BLK), :] = jnp.where(
                keep, mixed[:, :128] * inv, o_ref[pl.ds(at, BLK), :].astype(F32)).astype(BF16)
            l_ref[pl.ds(at, BLK), :] = jnp.where(keep, inv, l_ref[pl.ds(at, BLK), :])
            return carry

        lax.fori_loop(0, blocks, step, 0)

    for_each_picture(len_ref, off_ref, total, picture)


def attention_forward(lengths, offsets, q, k, v, code_q, code_k):
    total, width = q.shape
    pair = pl.BlockSpec((total, 128), lambda j, *_: (0, j))
    return pl.pallas_call(
        fwd_kernel,
        grid_spec=pltpu.PrefetchScalarGridSpec(
            num_scalar_prefetch=2,
            grid=(width // 128,),
            in_specs=[pair, pair, pair, const_spec((total, 128)), const_spec((total, 128))],
            out_specs=[pair, pair]),
        out_shape=[jax.ShapeDtypeStruct((total, width), BF16), jax.ShapeDtypeStruct((total, width), F32)],
        compiler_params=params(),
        name="attention_forward",
    )(lengths, offsets, q, k, v, code_q, code_k)


def bwd_kernel(len_ref, off_ref, q_ref, k_ref, v_ref, do_ref, da_ref, rq_ref, rk_ref, aq_ref, ak_ref,
               gq_ref, gk_ref, avg_ref,
               oq_ref, ok_ref, ov_ref, dgq_ref, dgk_ref,
               dq_ref, dk_ref, dv_ref, kt_ref, vt_ref):
    total = q_ref.shape[0]
    dq_ref[...] = jnp.zeros_like(dq_ref)
    dk_ref[...] = jnp.zeros_like(dk_ref)
    dv_ref[...] = jnp.zeros_like(dv_ref)
    left = half_masks(BLK)

    def picture(slot, start, stop, first, blocks):
        span = blocks * BLK
        keys_low = k_ref[pl.ds(first, span), :]
        keys = jnp.concatenate([keys_low, ak_ref[pl.ds(first, span), :]], axis=1)
        minus = jnp.full((span, 128), -1.0, BF16)
        vals = jnp.concatenate([v_ref[pl.ds(first, span), :], minus], axis=1)
        keys_st = stacked_heads(keys_low, half_masks(span))
        kt_ref[:, :span] = jnp.zeros((128, span), F32)
        vt_ref[:, :span] = jnp.zeros((128, span), F32)

        def step(j, carry):
            at = pl.multiple_of(first + j * BLK, 16)
            code = jnp.where(slot_lanes(slot, BLK), aq_ref[pl.ds(at, BLK), :], jnp.zeros((), BF16))
            query = stacked_heads(q_ref[pl.ds(at, BLK), :], left)
            grad = stacked_heads(do_ref[pl.ds(at, BLK), :], left)
            delta = stacked_heads(da_ref[pl.ds(at, BLK), :], left)
            weights = jnp.exp2(dot(jnp.concatenate([query, jnp.concatenate([code, code], axis=0)], axis=1), keys, NT))
            slope = dot(jnp.concatenate([grad, delta], axis=1), vals, NT)
            weights_low = weights.astype(BF16)
            scores = (weights * slope).astype(BF16)
            vt_ref[:, :span] += dot(grad, weights_low, TN)
            kt_ref[:, :span] += dot(query, scores, TN)
            wide = jnp.concatenate([scores[:BLK], scores[BLK:]], axis=1)
            new = dot(wide, keys_st)
            keep = inside_rows(at, start, stop, BLK, 128)
            dq_ref[pl.ds(at, BLK), :] = jnp.where(keep, new, dq_ref[pl.ds(at, BLK), :])
            return carry

        lax.fori_loop(0, blocks, step, 0)
        for j in range(blocks):
            at = pl.multiple_of(first + j * BLK, 16)
            keep = inside_rows(at, start, stop, BLK, 128)
            cols = slice(j * BLK, (j + 1) * BLK)
            dk_ref[pl.ds(at, BLK), :] = jnp.where(keep, kt_ref[:, cols].T, dk_ref[pl.ds(at, BLK), :])
            dv_ref[pl.ds(at, BLK), :] = jnp.where(keep, vt_ref[:, cols].T, dv_ref[pl.ds(at, BLK), :])

    for_each_picture(len_ref, off_ref, total, picture)

    avg = avg_ref[...]

    def norm_back(grad, low, gain, unit, rstd):
        z = low.astype(F32) * (1.0 / unit)
        inner = grad * gain
        mean = dot(inner.astype(BF16), avg)
        along = dot((inner * z).astype(BF16), avg)
        return rstd.astype(F32) * (inner - mean - z * along), jnp.sum(grad * z, axis=0, keepdims=True)

    sum_q = jnp.zeros((1, 128), F32)
    sum_k = jnp.zeros((1, 128), F32)
    rows = 512
    for r in range(0, total, rows):
        at = slice(r, r + rows)
        gain_q = gq_ref[...] * HD ** -0.5
        out, part = norm_back(dq_ref[at, :], q_ref[at, :], gain_q, gain_q * LOG2E, rq_ref[at, :])
        oq_ref[at, :] = out.astype(BF16)
        sum_q += part
        gain_k = gk_ref[...]
        out, part = norm_back(dk_ref[at, :] * LN2, k_ref[at, :], gain_k, gain_k, rk_ref[at, :])
        ok_ref[at, :] = out.astype(BF16)
        sum_k += part
        ov_ref[at, :] = dv_ref[at, :].astype(BF16)
    dgq_ref[...] = sum_q * HD ** -0.5
    dgk_ref[...] = sum_k


def attention_backward(lengths, offsets, q, k, v, grad, delta, rstd_q, rstd_k, code_q, code_k, gain_q, gain_k, avg):
    total, width = q.shape
    pair = pl.BlockSpec((total, 128), lambda j, *_: (0, j))
    vec = pl.BlockSpec((1, 128), lambda j, *_: (0, j))
    return pl.pallas_call(
        bwd_kernel,
        grid_spec=pltpu.PrefetchScalarGridSpec(
            num_scalar_prefetch=2,
            grid=(width // 128,),
            in_specs=[pair] * 7 + [const_spec((total, 128))] * 2 + [vec, vec, const_spec((128, 128))],
            out_specs=[pair] * 3 + [vec] * 2,
            scratch_shapes=[pltpu.VMEM((total, 128), F32)] * 3 + [pltpu.VMEM((128, MAX_BLOCKS * BLK), F32)] * 2),
        out_shape=[jax.ShapeDtypeStruct((total, width), BF16)] * 3 + [jax.ShapeDtypeStruct((1, width), F32)] * 2,
        compiler_params=params(),
        name="attention_backward",
    )(lengths, offsets, q, k, v, grad, delta, rstd_q, rstd_k, code_q, code_k, gain_q, gain_k, avg)


def gelu_pair(up):
    density = jnp.exp(-0.5 * (up * up))
    t = 1.0 / (1.0 + (0.3275911 * 0.7071067811865476) * jnp.abs(up))
    poly = 0.5 * 1.061405429
    for coef in (-1.453152027, 1.421413741, -0.284496736, 0.254829592):
        poly = poly * t + 0.5 * coef
    tail = poly * t * density
    return jnp.where(up >= 0, 1.0 - tail, tail), density * 0.3989422804014327


def mlp_kernel(perm_ref, x_ref, c_ref, m_ref, p_ref, l_ref, wo_ref, bo_ref, g2_ref, b2_ref, wu_ref, bu_ref, wd_ref,
               bd_ref, sum_ref,
               out_ref, gh_ref, do_ref, da_ref, dwo_ref, dwu_ref, dwd_ref, dbo_ref, dg2_ref, db2_ref, dbu_ref, dbd_ref,
               awo, awu, awd):
    step = pl.program_id(0)
    parts = perm_ref.shape[0]
    count = pl.num_programs(0) - parts
    width = x_ref.shape[1]
    hidden_width = wu_ref.shape[1]

    @pl.when(step == 0)
    def _():
        for ref in (awo, awu, awd, dbo_ref, dg2_ref, db2_ref, dbu_ref, dbd_ref):
            ref[...] = jnp.zeros(ref.shape, ref.dtype)

    @pl.when(step < count)
    def _():
        mixed = m_ref[...]
        hidden = x_ref[...].astype(F32) + dot(mixed, wo_ref[...]) + bo_ref[...]
        z, rstd = row_stats(hidden)
        normed = (z * g2_ref[...] + b2_ref[...]).astype(BF16)
        grad_out = c_ref[...].astype(F32) * p_ref[...]
        grad_low = grad_out.astype(BF16)
        out = hidden + bd_ref[...]
        grad_norm = jnp.zeros_like(hidden)
        for col in range(0, hidden_width, width):
            cols = slice(col, col + width)
            up = dot(normed, wu_ref[:, cols]) + bu_ref[:, cols]
            grad_act = dot(grad_low, wd_ref[cols, :], NT)
            phi, density = gelu_pair(up)
            act = (up * phi).astype(BF16)
            grad_up = grad_act * (phi + up * density)
            grad_up_low = grad_up.astype(BF16)
            out += dot(act, wd_ref[cols, :])
            awd[cols, :] += dot(act, grad_low, TN)
            awu[:, cols] += dot(normed, grad_up_low, TN)
            grad_norm += dot(grad_up_low, wu_ref[:, cols], NT)
            dbu_ref[:, cols] += jnp.sum(grad_up, axis=0, keepdims=True)
        out_ref[...] = out.astype(BF16)
        dbd_ref[...] += jnp.sum(grad_out, axis=0, keepdims=True)
        dg2_ref[...] += jnp.sum(grad_norm * z, axis=0, keepdims=True)
        db2_ref[...] += jnp.sum(grad_norm, axis=0, keepdims=True)
        inner = grad_norm * g2_ref[...]
        grad_hidden = grad_out + rstd * (inner - jnp.mean(inner, axis=-1, keepdims=True)
                                         - z * jnp.mean(inner * z, axis=-1, keepdims=True))
        gh_ref[...] = grad_hidden
        branch = grad_hidden.astype(BF16)
        dbo_ref[...] += jnp.sum(grad_hidden, axis=0, keepdims=True)
        awo[...] += dot(mixed, branch, TN)
        grad_mixed = dot(branch, wo_ref[...], NT)
        inv = l_ref[...]
        scaled = grad_mixed * inv
        do_ref[...] = scaled.astype(BF16)
        prod = scaled * mixed.astype(F32)
        high = prod.astype(BF16)
        low = (prod - high.astype(F32)).astype(BF16)
        lane = lax.broadcasted_iota(jnp.int32, (prod.shape[0], 256), 1) % HD
        for col in range(0, width, 256):
            cols = slice(col, col + 256)
            delta = dot(high[:, cols], sum_ref[...]) + dot(low[:, cols], sum_ref[...])
            first = delta.astype(BF16)
            rest = delta - first.astype(F32)
            da_ref[:, cols] = jnp.where(lane == 0, first.astype(F32), jnp.where(lane == 1, rest, 0.0)).astype(BF16)

    @pl.when(step >= count)
    def _():
        part = perm_ref[jnp.maximum(step - count, 0)]
        for acc, ref in ((awo, dwo_ref), (awu, dwu_ref), (awd, dwd_ref)):
            rows = ref.shape[0]
            ref[...] = acc[pl.ds(pl.multiple_of(part * rows, 16), rows), :].astype(BF16)


def mlp_both(perm, x, cot, mixed, pad, linv, wo, bo, g2, b2, wu, bu, wd, bd, summer):
    total, width = x.shape
    ff = wu.shape[1]
    parts = perm.shape[0]
    rows = 256
    count = total // rows
    tile = pl.BlockSpec((rows, width), lambda i, *_: (jnp.minimum(i, count - 1), 0))

    def grad_spec(shape):
        return pl.BlockSpec((shape[0] // parts, shape[1]), lambda i, *_: (jnp.maximum(i - count, 0), 0))

    vec = pl.BlockSpec((1, width), lambda i, *_: (0, 0))
    vec_ff = pl.BlockSpec((1, ff), lambda i, *_: (0, 0))
    return pl.pallas_call(
        mlp_kernel,
        grid_spec=pltpu.PrefetchScalarGridSpec(
            num_scalar_prefetch=1,
            grid=(count + parts,),
            in_specs=[tile, tile, tile, pl.BlockSpec((rows, 1), lambda i, *_: (jnp.minimum(i, count - 1), 0)), tile,
                      const_spec(wo.shape), const_spec((1, width)), const_spec((1, width)), const_spec((1, width)),
                      const_spec(wu.shape), const_spec((1, ff)), const_spec(wd.shape), const_spec((1, width)),
                      const_spec((256, 256))],
            out_specs=[tile, tile, tile, tile, grad_spec(wo.shape), grad_spec(wu.shape), grad_spec(wd.shape),
                       vec, vec, vec, vec_ff, vec],
            scratch_shapes=[pltpu.VMEM(wo.shape, F32), pltpu.VMEM(wu.shape, F32), pltpu.VMEM(wd.shape, F32)]),
        out_shape=[jax.ShapeDtypeStruct((total, width), BF16), jax.ShapeDtypeStruct((total, width), F32),
                   jax.ShapeDtypeStruct((total, width), BF16), jax.ShapeDtypeStruct((total, width), BF16),
                   jax.ShapeDtypeStruct(wo.shape, BF16), jax.ShapeDtypeStruct(wu.shape, BF16),
                   jax.ShapeDtypeStruct(wd.shape, BF16)]
        + [jax.ShapeDtypeStruct((1, n), F32) for n in (width, width, width, ff, width)],
        compiler_params=params(),
        name="mlp_both",
    )(perm, x, cot, mixed, pad, linv, wo, bo, g2, b2, wu, bu, wd, bd, summer)


def dqkv_kernel(perm_ref, n_ref, gq_ref, gk_ref, gv_ref, dw_ref, db_ref, acc):
    parts = perm_ref.shape[0]
    total, width = n_ref.shape
    rows = width // parts
    ones = jnp.ones((8, total), BF16)
    for i, ref in enumerate((gq_ref, gk_ref, gv_ref)):
        @pl.when(pl.program_id(0) == i)
        def _():
            acc[...] = dot(n_ref[...], ref[...], TN)
            db_ref[...] = dot(ones, ref[...])[:1]
    for part in range(parts):
        dw_ref[part * rows:(part + 1) * rows, :] = acc[
            pl.ds(pl.multiple_of(perm_ref[part] * rows, 8), rows), :].astype(BF16)


def qkv_weight_grad(perm, normed, gq, gk, gv):
    total, width = normed.shape
    return pl.pallas_call(
        dqkv_kernel,
        grid_spec=pltpu.PrefetchScalarGridSpec(
            num_scalar_prefetch=1,
            grid=(3,),
            in_specs=[const_spec((total, width))] * 4,
            out_specs=[pl.BlockSpec((width, width), lambda i, *_: (0, i)), pl.BlockSpec((1, width), lambda i, *_: (0, i))],
            scratch_shapes=[pltpu.VMEM((width, width), F32)]),
        out_shape=[jax.ShapeDtypeStruct((width, 3 * width), BF16), jax.ShapeDtypeStruct((1, 3 * width), F32)],
        compiler_params=params(),
        name="qkv_weight_grad",
    )(perm, normed, gq, gk, gv)


def dinput_kernel(x_ref, gh_ref, gq_ref, gk_ref, gv_ref, w_ref, g_ref, out_ref, dg_ref, db_ref):
    width = x_ref.shape[1]

    @pl.when(pl.program_id(0) == 0)
    def _():
        dg_ref[...] = jnp.zeros_like(dg_ref)
        db_ref[...] = jnp.zeros_like(db_ref)

    grad = dot(gq_ref[...], w_ref[:, :width], NT)
    grad += dot(gk_ref[...], w_ref[:, width:2 * width], NT)
    grad += dot(gv_ref[...], w_ref[:, 2 * width:], NT)
    z, rstd = row_stats(x_ref[...].astype(F32))
    dg_ref[...] += jnp.sum(grad * z, axis=0, keepdims=True)
    db_ref[...] += jnp.sum(grad, axis=0, keepdims=True)
    inner = grad * g_ref[...]
    out_ref[...] = gh_ref[...] + rstd * (inner - jnp.mean(inner, axis=-1, keepdims=True)
                                         - z * jnp.mean(inner * z, axis=-1, keepdims=True))


def input_grad(x, gh, gq, gk, gv, weight, gain):
    total, width = x.shape
    rows = 512
    tile = pl.BlockSpec((rows, width), lambda i: (i, 0))
    vec = pl.BlockSpec((1, width), lambda i: (0, 0))
    return pl.pallas_call(
        dinput_kernel,
        grid=(total // rows,),
        in_specs=[tile] * 5 + [const_spec(weight.shape), const_spec((1, width))],
        out_specs=[tile, vec, vec],
        out_shape=[jax.ShapeDtypeStruct((total, width), F32)] + [jax.ShapeDtypeStruct((1, width), F32)] * 2,
        compiler_params=params(),
        name="input_grad",
    )(x, gh, gq, gk, gv, weight, gain)


def gather(block):
    return lax.all_gather(block, "shard", axis=0, tiled=True)


def reduce_owned(grad):
    own = lax.psum_scatter(grad, "shard", scatter_dimension=0, tiled=True)
    return lax.psum(own, "rep").astype(F32)


PARTS = 8


def block_order():
    return jnp.arange(PARTS, dtype=jnp.int32)


def on_device(shards, reps, inputs, cotangent, picture_ids, picture_lengths, picture_offsets, padding, ln1_gain,
              ln1_bias, qkv_weight, qkv_bias, query_gain, key_gain, out_weight, out_bias, ln2_gain, ln2_bias,
              up_weight, up_bias, down_weight, down_bias):
    total, width = inputs.shape
    pairs = width // 128
    small = (ln1_gain, ln1_bias, qkv_bias, query_gain, key_gain, out_bias, ln2_gain, ln2_bias, up_bias, down_bias)
    sizes = [a.shape[0] for a in small]
    packed = gather(jnp.concatenate(small)[None])
    at = 0
    full = []
    for size in sizes:
        full.append(packed[:, at:at + size].reshape(1, shards * size).astype(F32))
        at += size
    gain_one, shift_one, bias_qkv, gain_query, gain_key, bias_out, gain_two, shift_two, bias_up, bias_down = full
    weight_qkv = gather(qkv_weight)
    weight_out = gather(out_weight)
    weight_up = gather(up_weight)
    weight_down = gather(down_weight)

    lengths = picture_lengths.reshape(-1)
    offsets = picture_offsets.reshape(-1)
    live = padding > 0
    lane = jnp.arange(128, dtype=jnp.int32)[None]
    held = ((picture_ids[:, None] == lane) & live[:, None]).astype(F32)
    last = (lane == CONST_LANE).astype(F32)
    code_q = (held + last).astype(BF16)
    code_k = ((held - last) * FAR).astype(BF16)
    head = jnp.arange(256, dtype=jnp.int32) // HD
    summer = (head[:, None] == head[None]).astype(BF16)
    avg = (summer.astype(F32) * (1.0 / HD)).astype(BF16)
    gain_q = jnp.tile(gain_query, (1, HEADS))
    gain_k = jnp.tile(gain_key, (1, HEADS))

    normed, q, k, v, rstd_q, rstd_k = qkv_project(
        inputs, gain_one, shift_one, weight_qkv, bias_qkv, gain_q * (HD ** -0.5 * LOG2E), gain_k, avg)
    mixed, linv = attention_forward(lengths, offsets, q, k, v, code_q, code_k)
    perm = block_order()
    (output, grad_hidden, grad_scaled, delta, dwo, dwu, dwd, dbo, dg2, db2, dbu, dbd) = mlp_both(
        perm, inputs, cotangent, mixed, padding.astype(F32)[:, None], linv, weight_out, bias_out, gain_two, shift_two,
        weight_up, bias_up, weight_down, bias_down, summer)
    own_down = reduce_owned(dwd)
    own_up = reduce_owned(dwu)
    own_out = reduce_owned(dwo)
    gq, gk, gv, dgq, dgk = attention_backward(
        lengths, offsets, q, k, v, grad_scaled, delta, rstd_q, rstd_k, code_q, code_k, gain_q, gain_k,
        avg[:128, :128])
    dw, db = qkv_weight_grad(perm, normed, gq, gk, gv)
    own_qkv = reduce_owned(dw)
    grad_input, dg1, db1 = input_grad(inputs, grad_hidden, gq, gk, gv, weight_qkv, gain_one)
    dgq = jnp.sum(dgq.reshape(HEADS, HD), axis=0)
    dgk = jnp.sum(dgk.reshape(HEADS, HD), axis=0)
    vectors = (dg1, db1, db, dgq, dgk, dbo, dg2, db2, dbu, dbd)
    rows = jnp.concatenate([g.reshape(shards, -1) for g in vectors], axis=1)
    own = reduce_owned(rows)[0]
    at = 0
    owned = []
    for size in sizes:
        owned.append(own[at:at + size])
        at += size
    og1, ob1, obqkv, ogq, ogk, obo, og2, ob2, obu, obd = owned
    return (output, grad_input, og1, ob1, own_qkv, obqkv, ogq, ogk, own_out, obo, og2, ob2, own_up, obu, own_down, obd)


def solution(mesh):
    rows2 = P(("rep", "shard"), None)
    rows1 = P(("rep", "shard"))
    vec, mat = P("shard"), P("shard", None)
    in_specs = (rows2, rows2, rows1, rows2, rows2, rows1, vec, vec, mat, vec, vec, vec, mat, vec, vec, vec, mat, vec,
                mat, vec)
    out_specs = (rows2, rows2, vec, vec, mat, vec, vec, vec, mat, vec, vec, vec, mat, vec, mat, vec)
    shards, reps = mesh.shape["shard"], mesh.shape["rep"]

    def body(*args):
        return on_device(shards, reps, *args)

    return jax.shard_map(body, mesh=mesh, in_specs=in_specs, out_specs=out_specs, check_vma=False)
```

```python
import functools

import jax
import jax.numpy as jnp
from jax import lax
from jax.experimental import pallas as pl
from jax.experimental.pallas import tpu as pltpu
from jax.sharding import PartitionSpec as P


HEADS = 12
HD = 64
NORM_EPS = 1e-06
LOG2E = 1.4426950408889634
LN2 = 0.6931471805599453
FAR = 512.0
CONST_LANE = 127
BLK = 256
MAX_BLOCKS = 5
VMEM_LIMIT = 60 * 1024 * 1024
PARTS = 8
SMALL = 16

F32 = jnp.float32
BF16 = jnp.bfloat16

NT = (((1,), (1,)), ((), ()))
NN = (((1,), (0,)), ((), ()))
TN = (((0,), (0,)), ((), ()))


def dot(lhs, rhs, dims=NN):
    return lax.dot_general(lhs, rhs, dims, preferred_element_type=F32)


def params(**kw):
    return pltpu.CompilerParams(vmem_limit_bytes=VMEM_LIMIT, **kw)


def cost(flops, traffic):
    return pl.CostEstimate(flops=int(flops), transcendentals=0, bytes_accessed=int(traffic))


def row_stats(values):
    mean = jnp.mean(values, axis=-1, keepdims=True)
    center = values - mean
    rstd = lax.rsqrt(jnp.mean(center * center, axis=-1, keepdims=True) + NORM_EPS)
    return center * rstd, rstd


def const_spec(shape):
    return pl.BlockSpec(shape, lambda *_: (0,) * len(shape), pipeline_mode=pl.Buffered(1))


def any_specs(count):
    return [pl.BlockSpec(memory_space=pl.ANY)] * count


class Laid:
    def __init__(self, pieces, coded):
        self.pieces, self.coded = pieces, coded

    def start(self, own, refs, dst, sem):
        for which, row, rows, place, col in self.pieces:
            ref = refs[which]
            if rows is None:
                pltpu.make_async_copy(ref, dst, sem).start()
                continue
            at = pl.multiple_of((own ^ place) * rows, 16) if self.coded else place * rows
            width = ref.shape[1]
            pltpu.make_async_copy(ref.at[pl.ds(row, rows), :],
                                  dst.at[pl.ds(at, rows), pl.ds(col * width, width)], sem).start()

    def wait(self, dst, sem):
        pltpu.make_async_copy(dst, dst, sem).wait()


def qkv_kernel(own_ref, *refs, count, laid):
    block_refs, refs = refs[:count], refs[count:]
    (x_ref, g_ref, b_ref, wb_ref, gq_ref, gk_ref, avg_ref, n_ref, q_ref, k_ref, v_ref, rq_ref, rk_ref, w_ref,
     sem) = refs

    @pl.when(pl.program_id(0) == 0)
    def _():
        laid.start(own_ref[0], block_refs, w_ref, sem)

    z, _ = row_stats(x_ref[...].astype(F32))
    n_ref[...] = (z * g_ref[...] + b_ref[...]).astype(BF16)

    @pl.when(pl.program_id(0) == 0)
    def _():
        laid.wait(w_ref, sem)

    normed = n_ref[...]
    avg = avg_ref[...]
    width = q_ref.shape[1]
    for part in range(3):
        for col in range(0, width, 256):
            here = slice(col, col + 256)
            cols = slice(part * width + col, part * width + col + 256)
            pre = dot(normed, w_ref[:, cols]) + wb_ref[:, cols]
            if part == 2:
                v_ref[:, here] = pre.astype(BF16)
                continue
            high = pre.astype(BF16)
            low = (pre - high.astype(F32)).astype(BF16)
            center = pre - (dot(high, avg) + dot(low, avg))
            rstd = lax.rsqrt(dot((center * center).astype(BF16), avg) + NORM_EPS)
            gain = gk_ref if part else gq_ref
            (k_ref if part else q_ref)[:, here] = (center * rstd * gain[:, here]).astype(BF16)
            (rk_ref if part else rq_ref)[:, here] = rstd.astype(BF16)


def qkv_project(own, weight, x, gain, bias, wbias, gain_q, gain_k, avg):
    blocks, laid = weight
    total, width = x.shape
    rows = 512
    tile = pl.BlockSpec((rows, width), lambda i, *_: (i, 0))
    vec = const_spec((1, width))
    return pl.pallas_call(
        functools.partial(qkv_kernel, count=len(blocks), laid=laid),
        grid_spec=pltpu.PrefetchScalarGridSpec(
            num_scalar_prefetch=1,
            grid=(total // rows,),
            in_specs=any_specs(len(blocks)) + [tile, vec, vec, const_spec((1, 3 * width)), vec, vec,
                                               const_spec((256, 256))],
            out_specs=[tile] * 6,
            scratch_shapes=[pltpu.VMEM((width, 3 * width), BF16), pltpu.SemaphoreType.DMA(())]),
        out_shape=[jax.ShapeDtypeStruct((total, width), BF16)] * 6,
        compiler_params=params(),
        cost_estimate=cost(6 * total * width * width, total * width * 14),
        name="qkv_project",
    )(own, *blocks, x, gain, bias, wbias, gain_q, gain_k, avg)


def half_masks(rows):
    lane = lax.broadcasted_iota(jnp.int32, (rows, 2 * HD), 1)
    return lane < HD


def for_each_picture(len_ref, off_ref, total, body):
    slots = len_ref.shape[0]

    def one(slot, carry):
        length = len_ref[slot]
        start = off_ref[slot]

        @pl.when(length > 0)
        def _():
            aligned = start // 16 * 16
            count = (start + length - aligned + BLK - 1) // BLK
            for blocks in range(1, MAX_BLOCKS + 1):
                @pl.when(count == blocks)
                def _():
                    first = pl.multiple_of(jnp.minimum(aligned, total - blocks * BLK), 16)
                    body(slot, start, start + length, first, blocks)

        return carry

    lax.fori_loop(0, slots, one, 0)


def inside_rows(first, start, stop, rows, width):
    at = first + lax.broadcasted_iota(jnp.int32, (rows, width), 0)
    return (at >= start) & (at < stop)


def stacked_heads(block, left):
    zero = jnp.zeros_like(block)
    return jnp.concatenate([jnp.where(left, block, zero), jnp.where(left, zero, block)], axis=0)


def slot_lanes(slot, rows):
    lane = lax.broadcasted_iota(jnp.int32, (rows, 128), 1)
    return (lane == slot) | (lane == CONST_LANE)


def fwd_kernel(len_ref, off_ref, q_ref, k_ref, v_ref, aq_ref, ak_ref, o_ref, e_ref, l_ref):
    total = q_ref.shape[0]
    o_ref[...] = v_ref[...]
    e_ref[...] = jnp.zeros_like(e_ref)
    l_ref[...] = jnp.zeros_like(l_ref)
    left = half_masks(BLK)
    one = jnp.ones((BLK, 128), BF16)

    def picture(slot, start, stop, first, blocks):
        span = blocks * BLK
        keys = jnp.concatenate([k_ref[pl.ds(first, span), :], ak_ref[pl.ds(first, span), :]], axis=1)
        vals = v_ref[pl.ds(first, span), :]
        left_all = half_masks(span)
        ones_all = jnp.ones((span, 128), BF16)
        vals = jnp.concatenate([stacked_heads(vals, left_all), stacked_heads(ones_all, left_all)], axis=1)

        def step(j, carry):
            at = pl.multiple_of(first + j * BLK, 16)
            code = jnp.where(slot_lanes(slot, BLK), aq_ref[pl.ds(at, BLK), :], jnp.zeros((), BF16))
            query = stacked_heads(q_ref[pl.ds(at, BLK), :], left)
            query = jnp.concatenate([query, jnp.concatenate([code, code], axis=0)], axis=1)
            shares = jnp.exp2(dot(query, keys, NT)).astype(BF16)
            shares = jnp.concatenate([shares[:BLK], shares[BLK:]], axis=1)
            mixed = dot(shares, vals)
            keep = inside_rows(at, start, stop, BLK, 128)
            inv = 1.0 / mixed[:, 128:]
            out = mixed[:, :128] * inv
            high = out.astype(BF16)
            rest = out - high.astype(F32)
            o_ref[pl.ds(at, BLK), :] = jnp.where(keep, high, o_ref[pl.ds(at, BLK), :])
            e_ref[pl.ds(at, BLK), :] = jnp.where(keep, rest.astype(BF16), e_ref[pl.ds(at, BLK), :])
            l_ref[pl.ds(at, BLK), :] = jnp.where(keep, inv, l_ref[pl.ds(at, BLK), :])
            return carry

        lax.fori_loop(0, blocks, step, 0)

    for_each_picture(len_ref, off_ref, total, picture)


def attention_forward(lengths, offsets, q, k, v, code_q, code_k):
    total, width = q.shape
    pair = pl.BlockSpec((total, 128), lambda j, *_: (0, j))
    return pl.pallas_call(
        fwd_kernel,
        grid_spec=pltpu.PrefetchScalarGridSpec(
            num_scalar_prefetch=2,
            grid=(width // 128,),
            in_specs=[pair, pair, pair, const_spec((total, 128)), const_spec((total, 128))],
            out_specs=[pair] * 3),
        out_shape=[jax.ShapeDtypeStruct((total, width), BF16)] * 2 + [jax.ShapeDtypeStruct((total, width), F32)],
        compiler_params=params(),
        cost_estimate=cost(5 * total * total * width, total * width * 14),
        name="attention_forward",
    )(lengths, offsets, q, k, v, code_q, code_k)


def bwd_kernel(len_ref, off_ref, q_ref, k_ref, v_ref, do_ref, da_ref, rq_ref, rk_ref, aq_ref, ak_ref,
               gq_ref, gk_ref, avg_ref,
               oq_ref, ok_ref, ov_ref, dgq_ref, dgk_ref,
               dq_ref, dk_ref, dv_ref, kt_ref, vt_ref):
    total = q_ref.shape[0]
    dq_ref[...] = jnp.zeros_like(dq_ref)
    dk_ref[...] = jnp.zeros_like(dk_ref)
    dv_ref[...] = jnp.zeros_like(dv_ref)
    left = half_masks(BLK)

    def picture(slot, start, stop, first, blocks):
        span = blocks * BLK
        keys_low = k_ref[pl.ds(first, span), :]
        keys = jnp.concatenate([keys_low, ak_ref[pl.ds(first, span), :]], axis=1)
        minus = jnp.full((span, 128), -1.0, BF16)
        vals = jnp.concatenate([v_ref[pl.ds(first, span), :], minus], axis=1)
        keys_st = stacked_heads(keys_low, half_masks(span))
        kt_ref[:, :span] = jnp.zeros((128, span), F32)
        vt_ref[:, :span] = jnp.zeros((128, span), F32)

        def step(j, carry):
            at = pl.multiple_of(first + j * BLK, 16)
            code = jnp.where(slot_lanes(slot, BLK), aq_ref[pl.ds(at, BLK), :], jnp.zeros((), BF16))
            query = stacked_heads(q_ref[pl.ds(at, BLK), :], left)
            grad = stacked_heads(do_ref[pl.ds(at, BLK), :], left)
            delta = stacked_heads(da_ref[pl.ds(at, BLK), :], left)
            weights = jnp.exp2(dot(jnp.concatenate([query, jnp.concatenate([code, code], axis=0)], axis=1), keys, NT))
            slope = dot(jnp.concatenate([grad, delta], axis=1), vals, NT)
            weights_low = weights.astype(BF16)
            scores = (weights * slope).astype(BF16)
            vt_ref[:, :span] += dot(grad, weights_low, TN)
            kt_ref[:, :span] += dot(query, scores, TN)
            wide = jnp.concatenate([scores[:BLK], scores[BLK:]], axis=1)
            new = dot(wide, keys_st)
            keep = inside_rows(at, start, stop, BLK, 128)
            dq_ref[pl.ds(at, BLK), :] = jnp.where(keep, new, dq_ref[pl.ds(at, BLK), :])
            return carry

        lax.fori_loop(0, blocks, step, 0)
        for j in range(blocks):
            at = pl.multiple_of(first + j * BLK, 16)
            keep = inside_rows(at, start, stop, BLK, 128)
            cols = slice(j * BLK, (j + 1) * BLK)
            dk_ref[pl.ds(at, BLK), :] = jnp.where(keep, kt_ref[:, cols].T, dk_ref[pl.ds(at, BLK), :])
            dv_ref[pl.ds(at, BLK), :] = jnp.where(keep, vt_ref[:, cols].T, dv_ref[pl.ds(at, BLK), :])

    for_each_picture(len_ref, off_ref, total, picture)

    avg = avg_ref[...]

    def norm_back(grad, low, gain, unit, rstd):
        z = low.astype(F32) * (1.0 / unit)
        inner = grad * gain
        mean = dot(inner.astype(BF16), avg)
        along = dot((inner * z).astype(BF16), avg)
        return rstd.astype(F32) * (inner - mean - z * along), jnp.sum(grad * z, axis=0, keepdims=True)

    sum_q = jnp.zeros((1, 128), F32)
    sum_k = jnp.zeros((1, 128), F32)
    rows = 512
    for r in range(0, total, rows):
        at = slice(r, r + rows)
        gain_q = gq_ref[...] * HD ** -0.5
        out, part = norm_back(dq_ref[at, :], q_ref[at, :], gain_q, gain_q * LOG2E, rq_ref[at, :])
        oq_ref[at, :] = out.astype(BF16)
        sum_q += part
        gain_k = gk_ref[...]
        out, part = norm_back(dk_ref[at, :] * LN2, k_ref[at, :], gain_k, gain_k, rk_ref[at, :])
        ok_ref[at, :] = out.astype(BF16)
        sum_k += part
        ov_ref[at, :] = dv_ref[at, :].astype(BF16)
    dgq_ref[...] = sum_q * HD ** -0.5
    dgk_ref[...] = sum_k


def attention_backward(lengths, offsets, q, k, v, grad, delta, rstd_q, rstd_k, code_q, code_k, gain_q, gain_k, avg):
    total, width = q.shape
    pair = pl.BlockSpec((total, 128), lambda j, *_: (0, j))
    vec = pl.BlockSpec((1, 128), lambda j, *_: (0, j))
    return pl.pallas_call(
        bwd_kernel,
        grid_spec=pltpu.PrefetchScalarGridSpec(
            num_scalar_prefetch=2,
            grid=(width // 128,),
            in_specs=[pair] * 7 + [const_spec((total, 128))] * 2 + [vec, vec, const_spec((128, 128))],
            out_specs=[pair] * 3 + [vec] * 2,
            scratch_shapes=[pltpu.VMEM((total, 128), F32)] * 3 + [pltpu.VMEM((128, MAX_BLOCKS * BLK), F32)] * 2),
        out_shape=[jax.ShapeDtypeStruct((total, width), BF16)] * 3 + [jax.ShapeDtypeStruct((1, width), F32)] * 2,
        compiler_params=params(),
        cost_estimate=cost(8 * total * total * width, total * width * 20),
        name="attention_backward",
    )(lengths, offsets, q, k, v, grad, delta, rstd_q, rstd_k, code_q, code_k, gain_q, gain_k, avg)


def gelu_pair(up):
    density = jnp.exp(-0.5 * (up * up))
    t = 1.0 / (1.0 + (0.3275911 * 0.7071067811865476) * jnp.abs(up))
    poly = 0.5 * 1.061405429
    for coef in (-1.453152027, 1.421413741, -0.284496736, 0.254829592):
        poly = poly * t + 0.5 * coef
    tail = poly * t * density
    return jnp.where(up >= 0, 1.0 - tail, tail), density * 0.3989422804014327


def mlp_kernel(*refs, count_w, laid):
    block_refs, refs = refs[:count_w], refs[count_w:]
    (x_ref, c_ref, m_ref, e_ref, l_ref, p_ref, bo_ref, g2_ref, b2_ref, bu_ref, bd_ref, sum_ref,
     out_ref, gh_ref, do_ref, da_ref, dw_ref, dbo_ref, dg2_ref, db2_ref, dbu_ref, dbd_ref,
     awo, awu, awd, wo_ref, wu_ref, wd_ref, sems) = refs
    step = pl.program_id(0)
    count = pl.num_programs(0) - PARTS
    width = x_ref.shape[1]
    hidden_width = wd_ref.shape[0]

    @pl.when(step == 0)
    def _():
        for i, (part, dst) in enumerate(zip(laid, (wo_ref, wu_ref, wd_ref))):
            part.start(0, block_refs, dst, sems.at[i])
        for ref in (awo, awu, awd, dbo_ref, dg2_ref, db2_ref, dbu_ref, dbd_ref):
            ref[...] = jnp.zeros(ref.shape, ref.dtype)
        for i, (part, dst) in enumerate(zip(laid, (wo_ref, wu_ref, wd_ref))):
            part.wait(dst, sems.at[i])

    @pl.when(step < count)
    def _():
        mixed = m_ref[...]
        hidden = x_ref[...].astype(F32) + dot(mixed, wo_ref[...]) + bo_ref[...]
        z, rstd = row_stats(hidden)
        normed = (z * g2_ref[...] + b2_ref[...]).astype(BF16)
        grad_out = c_ref[...].astype(F32) * p_ref[...]
        grad_low = grad_out.astype(BF16)
        out = hidden + bd_ref[...]
        grad_norm = jnp.zeros_like(hidden)
        for col in range(0, hidden_width, width):
            cols = slice(col, col + width)
            up = dot(normed, wu_ref[:, cols]) + bu_ref[:, cols]
            grad_act = dot(grad_low, wd_ref[cols, :], NT)
            phi, density = gelu_pair(up)
            act = (up * phi).astype(BF16)
            grad_up = grad_act * (phi + up * density)
            grad_up_low = grad_up.astype(BF16)
            out += dot(act, wd_ref[cols, :])
            awd[cols, :] += dot(act, grad_low, TN)
            awu[:, cols] += dot(normed, grad_up_low, TN)
            grad_norm += dot(grad_up_low, wu_ref[:, cols], NT)
            dbu_ref[:, cols] += jnp.sum(grad_up, axis=0, keepdims=True)
        out_ref[...] = out.astype(BF16)
        dbd_ref[...] += jnp.sum(grad_out, axis=0, keepdims=True)
        dg2_ref[...] += jnp.sum(grad_norm * z, axis=0, keepdims=True)
        db2_ref[...] += jnp.sum(grad_norm, axis=0, keepdims=True)
        inner = grad_norm * g2_ref[...]
        grad_hidden = grad_out + rstd * (inner - jnp.mean(inner, axis=-1, keepdims=True)
                                         - z * jnp.mean(inner * z, axis=-1, keepdims=True))
        gh_ref[...] = grad_hidden
        branch = grad_hidden.astype(BF16)
        dbo_ref[...] += jnp.sum(grad_hidden, axis=0, keepdims=True)
        awo[...] += dot(mixed, branch, TN)
        grad_mixed = dot(branch, wo_ref[...], NT)
        scaled = (grad_mixed * l_ref[...]).astype(BF16)
        do_ref[...] = scaled
        prod = scaled.astype(F32) * (mixed.astype(F32) + e_ref[...].astype(F32))
        high = prod.astype(BF16)
        low = (prod - high.astype(F32)).astype(BF16)
        lane = lax.broadcasted_iota(jnp.int32, (prod.shape[0], 256), 1) % HD
        for col in range(0, width, 256):
            cols = slice(col, col + 256)
            delta = dot(high[:, cols], sum_ref[...]) + dot(low[:, cols], sum_ref[...])
            first = delta.astype(BF16)
            rest = delta - first.astype(F32)
            da_ref[:, cols] = jnp.where(lane == 0, first.astype(F32), jnp.where(lane == 1, rest, 0.0)).astype(BF16)

    @pl.when(step >= count)
    def _():
        part = jnp.maximum(step - count, 0)
        short, tall = width // PARTS, hidden_width // PARTS
        narrow = pl.ds(pl.multiple_of(part * short, 16), short)
        dw_ref[:short, :] = awo[narrow, :].astype(BF16)
        for i in range(hidden_width // width):
            dw_ref[(i + 1) * short:(i + 2) * short, :] = awu[narrow, i * width:(i + 1) * width].astype(BF16)
        dw_ref[dw_ref.shape[0] - tall:, :] = awd[pl.ds(pl.multiple_of(part * tall, 16), tall), :].astype(BF16)


def mlp_both(weight, x, cot, mixed, rest, linv, pad, bo, g2, b2, bu, bd, summer):
    blocks, laid = weight
    total, width = x.shape
    ff = bu.shape[1]
    rows = 256
    count = total // rows

    def row_spec(cols):
        return pl.BlockSpec((rows, cols), lambda i: (jnp.minimum(i, count - 1), 0))

    shapes = ((width, width), (width, ff), (ff, width))
    vectors = (width, width, width, ff, width)
    tile = row_spec(width)
    vec = const_spec((1, width))
    each = (width + 2 * ff) // PARTS
    return pl.pallas_call(
        functools.partial(mlp_kernel, count_w=len(blocks), laid=laid),
        grid=(count + PARTS,),
        in_specs=any_specs(len(blocks)) + [tile] * 5 + [row_spec(1), vec, vec, vec, const_spec((1, ff)), vec,
                                                        const_spec((256, 256))],
        out_specs=[tile] * 4 + [pl.BlockSpec((each, width), lambda i: (jnp.maximum(i - count, 0), 0))]
        + [pl.BlockSpec((1, n), lambda i: (0, 0)) for n in vectors],
        scratch_shapes=[pltpu.VMEM(s, F32) for s in shapes] + [pltpu.VMEM(s, BF16) for s in shapes] + [
            pltpu.SemaphoreType.DMA((3,))],
        out_shape=[jax.ShapeDtypeStruct((total, width), BF16), jax.ShapeDtypeStruct((total, width), F32)]
        + [jax.ShapeDtypeStruct((total, width), BF16)] * 2
        + [jax.ShapeDtypeStruct((each * PARTS, width), BF16)]
        + [jax.ShapeDtypeStruct((1, n), F32) for n in vectors],
        compiler_params=params(),
        cost_estimate=cost(2 * total * width * (3 * width + 6 * ff), total * width * 24),
        name="mlp_both",
    )(*blocks, x, cot, mixed, rest, linv, pad, bo, g2, b2, bu, bd, summer)


def dqkv_kernel(perm_ref, n_ref, gq_ref, gk_ref, gv_ref, *refs, counts, sizes):
    vectors, (send_ref, keep_ref, acc, boxes) = refs[:-4], refs[-4:]
    total, width = n_ref.shape
    rows = width // PARTS
    half = PARTS // 2
    each = 3 * rows + SMALL
    ones = jnp.ones((8, total), BF16)
    parts = (gq_ref, gk_ref, gv_ref)
    for i, ref in enumerate(parts):
        acc[:, i * width:(i + 1) * width] = dot(n_ref[...], ref[...], TN)
    bias = jnp.concatenate([dot(ones, ref[...])[:1] for ref in parts], axis=1)
    boxes[...] = jnp.zeros_like(boxes)
    at = 0
    for i, (count, size) in enumerate(zip(counts, sizes)):
        whole = bias if count == 0 else vectors[at][...]
        at += count
        span = size * PARTS
        fold = whole[:, :span]
        for extra in range(span, whole.shape[1], span):
            fold = fold + whole[:, extra:extra + span]
        for a in range(PARTS):
            boxes[a, i:i + 1, :size] = fold[:, a * size:(a + 1) * size]
    for part in range(PARTS):
        out = keep_ref if part >= half else send_ref
        place = perm_ref[part]
        at = (part % half) * each
        for i in range(3):
            out[at + i * rows:at + (i + 1) * rows, :] = acc[
                pl.ds(pl.multiple_of(place * rows, 8), rows), i * width:(i + 1) * width].astype(BF16)
        out[at + 3 * rows:at + each, :] = boxes[place].astype(BF16)


def qkv_weight_grad(perm, normed, gq, gk, gv, vectors, sizes):
    total, width = normed.shape
    vmem = pl.BlockSpec(memory_space=pltpu.VMEM)
    given = [v for v in vectors if v is not None]
    each = 3 * width // PARTS + SMALL
    return pl.pallas_call(
        functools.partial(dqkv_kernel, counts=[int(v is not None) for v in vectors], sizes=sizes),
        grid_spec=pltpu.PrefetchScalarGridSpec(
            num_scalar_prefetch=1,
            grid=(),
            in_specs=[vmem] * (4 + len(given)),
            out_specs=[vmem] * 2,
            scratch_shapes=[pltpu.VMEM((width, 3 * width), F32), pltpu.VMEM((PARTS, SMALL, width), F32)]),
        out_shape=[jax.ShapeDtypeStruct((each * PARTS // 2, width), BF16)] * 2,
        compiler_params=params(),
        cost_estimate=cost(6 * total * width * width, total * width * 8),
        name="qkv_weight_grad",
    )(perm, normed, gq, gk, gv, *given)


def dinput_kernel(own_ref, *refs, count, laid):
    block_refs, refs = refs[:count], refs[count:]
    gq_ref, gk_ref, gv_ref, x_ref, gh_ref, g_ref, out_ref, dg_ref, db_ref, w_ref, sem = refs
    width = x_ref.shape[1]

    @pl.when(pl.program_id(0) == 0)
    def _():
        laid.start(own_ref[0], block_refs, w_ref, sem)
        dg_ref[...] = jnp.zeros_like(dg_ref)
        db_ref[...] = jnp.zeros_like(db_ref)
        laid.wait(w_ref, sem)

    grad = dot(gq_ref[...], w_ref[:, :width], NT)
    grad += dot(gk_ref[...], w_ref[:, width:2 * width], NT)
    grad += dot(gv_ref[...], w_ref[:, 2 * width:], NT)
    z, rstd = row_stats(x_ref[...].astype(F32))
    dg_ref[...] += jnp.sum(grad * z, axis=0, keepdims=True)
    db_ref[...] += jnp.sum(grad, axis=0, keepdims=True)
    inner = grad * g_ref[...]
    out_ref[...] = gh_ref[...] + rstd * (inner - jnp.mean(inner, axis=-1, keepdims=True)
                                         - z * jnp.mean(inner * z, axis=-1, keepdims=True))


def input_grad(own, weight, gq, gk, gv, x, gh, gain):
    blocks, laid = weight
    total, width = x.shape
    rows = 512
    tile = pl.BlockSpec((rows, width), lambda i, *_: (i, 0))
    vec = pl.BlockSpec((1, width), lambda i, *_: (0, 0))
    return pl.pallas_call(
        functools.partial(dinput_kernel, count=len(blocks), laid=laid),
        grid_spec=pltpu.PrefetchScalarGridSpec(
            num_scalar_prefetch=1,
            grid=(total // rows,),
            in_specs=any_specs(len(blocks)) + [tile] * 5 + [const_spec((1, width))],
            out_specs=[tile, vec, vec],
            scratch_shapes=[pltpu.VMEM((width, 3 * width), BF16), pltpu.SemaphoreType.DMA(())]),
        out_shape=[jax.ShapeDtypeStruct((total, width), F32)] + [jax.ShapeDtypeStruct((1, width), F32)] * 2,
        compiler_params=params(),
        cost_estimate=cost(6 * total * width * width, total * width * 16),
        name="input_grad",
    )(own, *blocks, gq, gk, gv, x, gh, gain)


def pack_kernel(w_ref, *refs):
    out = refs[-1]
    rows = w_ref.shape[0]
    width = out.shape[1]
    for i in range(3):
        out[i * rows:(i + 1) * rows, :] = w_ref[:, i * width:(i + 1) * width]
    box = jnp.zeros((1, width), F32)
    out[3 * rows:, :] = jnp.zeros((SMALL, width), BF16)
    for i, ref in enumerate(refs[:-1]):
        out[3 * rows + i:3 * rows + i + 1, :ref.shape[1]] = ref[...]


def pack_share(weight, vectors):
    rows, width = weight.shape[0], weight.shape[1] // 3
    return pl.pallas_call(
        pack_kernel, out_shape=jax.ShapeDtypeStruct((3 * rows + SMALL, width), BF16), name="pack_share",
    )(weight, *[v[None] for v in vectors])


def unpack_kernel(own_ref, *refs, sizes, codes):
    blocks, outs, box = refs[:len(codes)], refs[len(codes):-1], refs[-1]
    for code, ref in zip(codes, blocks):
        box[own_ref[0] ^ code] = ref[...].astype(F32)
    for a in range(PARTS):
        block = box[a]
        for i, (size, out) in enumerate(zip(sizes, outs)):
            out[:, a * size:(a + 1) * size] = block[i:i + 1, :size]


def unpack_small(own, blocks, places, sizes):
    width = blocks[0].shape[1]

    def spec(row):
        return pl.BlockSpec((SMALL, width), lambda i, *_: (row // SMALL, 0))

    return pl.pallas_call(
        functools.partial(unpack_kernel, sizes=sizes, codes=[c for _, _, c in places]),
        grid_spec=pltpu.PrefetchScalarGridSpec(
            num_scalar_prefetch=1, grid=(1,), in_specs=[spec(row) for _, row, _ in places],
            out_specs=[pl.BlockSpec((1, PARTS * n), lambda i, *_: (0, 0)) for n in sizes],
            scratch_shapes=[pltpu.VMEM((PARTS, SMALL, width), F32)]),
        out_shape=[jax.ShapeDtypeStruct((1, PARTS * n), F32) for n in sizes],
        name="unpack_small",
    )(own, *[blocks[which] for which, _, _ in places])


def swap(value, code):
    return lax.ppermute(value, "shard", [(i, i ^ code) for i in range(8)])


def swap_mixed(value, even, odd):
    return lax.ppermute(value, "shard", [(i, i ^ (odd if i % 2 else even)) for i in range(8)])


def along(value, pairs):
    return lax.ppermute(value, "rep", pairs)


def total_of(*values):
    out = values[0].astype(F32)
    for value in values[1:]:
        out = out + value.astype(F32)
    return out


class Chips:
    def __init__(self):
        self.own = lax.axis_index("shard").astype(jnp.int32)
        self.rep = lax.axis_index("rep")
        odd = self.own % 2 == 1
        first = jnp.array([1, 3, 5, 7, 0, 4, 2, 6], jnp.int32)
        second = jnp.array([1, 5, 3, 7, 0, 2, 4, 6], jnp.int32)
        self.perm = jnp.where(odd, second, first) ^ self.own

    def gather_share(self, weight, vectors, sizes):
        share = pack_share(weight, vectors)
        each = share.shape[0]
        rows = weight.shape[0]
        right, up, far = swap(share, 2), swap(share, 4), swap(share, 6)
        self.fence = far
        others = swap(jnp.concatenate([share, right, up, far], axis=0), 1)
        blocks = [share, right, up, far, others]
        starts = [(0, 0, 0), (1, 0, 2), (2, 0, 4), (3, 0, 6)] + [(4, i * each, c) for i, c in enumerate((1, 3, 5, 7))]
        laid = Laid([(w, r + i * rows, rows, c, i) for w, r, c in starts for i in range(3)], True)
        small = unpack_small(self.own[None], blocks, [(w, r + 3 * rows, c) for w, r, c in starts], sizes)
        return (blocks, laid), small

    def gather_rest(self, wo, wu, wd):
        rows, width = wo.shape
        tall = wd.shape[0]
        cuts = wu.shape[1] // width
        share = jnp.concatenate([wo] + [wu[:, i * width:(i + 1) * width] for i in range(cuts)] + [wd], axis=0)
        each = share.shape[0]
        share, _ = lax.optimization_barrier((share, self.fence))
        whole = lax.all_gather(share, "shard", axis=0, tiled=True)
        laid_o = Laid([(0, a * each, rows, a, 0) for a in range(PARTS)], False)
        laid_u = Laid([(0, a * each + (i + 1) * rows, rows, a, i) for a in range(PARTS) for i in range(cuts)], False)
        laid_d = Laid([(0, (a + 1) * each - tall, tall, a, 0) for a in range(PARTS)], False)
        return [whole], (laid_o, laid_u, laid_d)

    def reduce_rest(self, stacked, width, ff):
        own = lax.psum_scatter(stacked, "shard", scatter_dimension=0, tiled=True)
        own = lax.psum(own, "rep")
        rows, cuts, tall = width // PARTS, ff // width, ff // PARTS
        own = own.astype(F32)
        up = jnp.concatenate([own[(i + 1) * rows:(i + 2) * rows] for i in range(cuts)], axis=1)
        return own[:rows], up, own[own.shape[0] - tall:]

    def reduce_share(self, send, keep, sizes):
        rows = keep.shape[0] // 4
        got = swap(send, 1)
        tail = total_of(keep[2 * rows:], got[2 * rows:]).astype(BF16)
        more = swap_mixed(tail, 2, 4)
        near = total_of(keep[rows:2 * rows], got[rows:2 * rows], more[rows:]).astype(BF16)
        last = swap_mixed(near, 4, 2)
        mine = total_of(keep[:rows], got[:rows], more[:rows], last).astype(BF16)
        inner = total_of(mine, along(mine, [(0, 1), (3, 2)])).astype(BF16)
        whole = total_of(inner, along(inner, [(1, 2), (2, 1)])).astype(BF16)
        outer = along(whole, [(1, 0), (2, 3)])
        own = jnp.where((self.rep == 0) | (self.rep == 3), outer, whole).astype(F32)
        cut = (rows - SMALL) // 3
        weight = jnp.concatenate([own[i * cut:(i + 1) * cut] for i in range(3)], axis=1)
        return weight, [own[3 * cut + i, :n] for i, n in enumerate(sizes)]


class Anywhere:
    def __init__(self, shards):
        self.shards = shards
        self.own = jnp.zeros((), jnp.int32)
        self.perm = jnp.arange(PARTS, dtype=jnp.int32)

    def gather(self, value):
        return lax.all_gather(value, "shard", axis=0, tiled=True)

    def gather_share(self, weight, vectors, sizes):
        small = [self.gather(v).astype(F32)[None] for v in vectors]
        return ([self.gather(weight)], Laid([(0, 0, None, 0, 0)], True)), small

    def gather_rest(self, wo, wu, wd):
        return [self.gather(w) for w in (wo, wu, wd)], tuple(Laid([(i, 0, None, 0, 0)], False) for i in range(3))

    def reduce(self, grad):
        return lax.psum(lax.psum_scatter(grad, "shard", scatter_dimension=0, tiled=True), "rep").astype(F32)

    def reduce_rest(self, stacked, width, ff):
        rows, cuts, tall = width // PARTS, ff // width, ff // PARTS
        each = stacked.reshape(PARTS, -1, width)
        up = jnp.concatenate([each[:, (i + 1) * rows:(i + 2) * rows].reshape(width, width) for i in range(cuts)], axis=1)
        out = each[:, :rows].reshape(width, width)
        return self.reduce(out), self.reduce(up), self.reduce(each[:, each.shape[1] - tall:].reshape(ff, width))

    def reduce_share(self, send, keep, sizes):
        width = send.shape[1]
        each = jnp.concatenate([send, keep], axis=0).reshape(PARTS, -1, width)
        cut = (each.shape[1] - SMALL) // 3
        weight = jnp.concatenate([each[:, i * cut:(i + 1) * cut].reshape(width, width) for i in range(3)], axis=1)
        small = [self.reduce(each[:, 3 * cut + i, :n * self.shards // PARTS].reshape(-1)) for i, n in enumerate(sizes)]
        return self.reduce(weight), small


def on_device(shards, reps, inputs, cotangent, picture_ids, picture_lengths, picture_offsets, padding, ln1_gain,
              ln1_bias, qkv_weight, qkv_bias, query_gain, key_gain, out_weight, out_bias, ln2_gain, ln2_bias,
              up_weight, up_bias, down_weight, down_bias):
    _, width = inputs.shape
    chips = Chips() if (shards, reps) == (PARTS, 4) else Anywhere(shards)
    own = chips.own[None]
    small = (ln1_gain, ln1_bias, qkv_bias, query_gain, key_gain, out_bias, ln2_gain, ln2_bias, up_bias, down_bias)
    sizes = tuple(a.shape[0] for a in small)
    weight_qkv, full = chips.gather_share(qkv_weight, small, sizes)
    weight_rest = chips.gather_rest(out_weight, up_weight, down_weight)
    gain_one, shift_one, bias_qkv, gain_query, gain_key, bias_out, gain_two, shift_two, bias_up, bias_down = full

    lengths = picture_lengths.reshape(-1)
    offsets = picture_offsets.reshape(-1)
    live = padding > 0
    lane = jnp.arange(128, dtype=jnp.int32)[None]
    held = ((picture_ids[:, None] == lane) & live[:, None]).astype(F32)
    last = (lane == CONST_LANE).astype(F32)
    code_q = (held + last).astype(BF16)
    code_k = ((held - last) * FAR).astype(BF16)
    head = jnp.arange(256, dtype=jnp.int32) // HD
    summer = (head[:, None] == head[None]).astype(BF16)
    avg = (summer.astype(F32) * (1.0 / HD)).astype(BF16)
    gain_q = jnp.tile(gain_query, (1, HEADS))
    gain_k = jnp.tile(gain_key, (1, HEADS))

    normed, q, k, v, rstd_q, rstd_k = qkv_project(
        own, weight_qkv, inputs, gain_one, shift_one, bias_qkv, gain_q * (HD ** -0.5 * LOG2E), gain_k, avg)
    mixed, mixed_rest, linv = attention_forward(lengths, offsets, q, k, v, code_q, code_k)
    output, grad_hidden, scaled, delta, stacked, dbo, dg2, db2, dbu, dbd = mlp_both(
        weight_rest, inputs, cotangent, mixed, mixed_rest, linv, padding.astype(F32)[:, None], bias_out, gain_two,
        shift_two, bias_up, bias_down, summer)
    own_out, own_up, own_down = chips.reduce_rest(stacked, width, bias_up.shape[1])
    gq, gk, gv, dgq, dgk = attention_backward(
        lengths, offsets, q, k, v, scaled, delta, rstd_q, rstd_k, code_q, code_k, gain_q, gain_k, avg[:128, :128])
    grad_input, dg1, db1 = input_grad(own, weight_qkv, gq, gk, gv, inputs, grad_hidden, gain_one)
    send, keep = qkv_weight_grad(
        chips.perm, normed, gq, gk, gv, (dg1, db1, None, dgq, dgk, dbo, dg2, db2, dbu, dbd),
        tuple(n * shards // PARTS for n in sizes))
    own_qkv, owned = chips.reduce_share(send, keep, sizes)
    og1, ob1, obqkv, ogq, ogk, obo, og2, ob2, obu, obd = owned
    return (output, grad_input, og1, ob1, own_qkv, obqkv, ogq, ogk, own_out, obo, og2, ob2, own_up, obu, own_down, obd)


def solution(mesh):
    rows2 = P(("rep", "shard"), None)
    rows1 = P(("rep", "shard"))
    vec, mat = P("shard"), P("shard", None)
    in_specs = (rows2, rows2, rows1, rows2, rows2, rows1, vec, vec, mat, vec, vec, vec, mat, vec, vec, vec, mat, vec,
                mat, vec)
    out_specs = (rows2, rows2, vec, vec, mat, vec, vec, vec, mat, vec, vec, vec, mat, vec, mat, vec)
    shards, reps = mesh.shape["shard"], mesh.shape["rep"]

    def body(*args):
        return on_device(shards, reps, *args)

    return jax.shard_map(body, mesh=mesh, in_specs=in_specs, out_specs=out_specs, check_vma=False)
```
